32 devices in a mesh: nodes: 16 (over z, y, x), tower: 2 (over core).
Axes of the slice: x: 2, y: 2, z: 4, core: 2. Of those that a mesh axis runs over, the one named last changes fastest.
Arguments:
- features: bfloat16 [16384, 128], P('nodes'), may hold values from -6 to 6
- edge_values: bfloat16 [16384, 256], P('nodes'), may hold values from -6 to 6
- degree: int32 [16384], P('nodes'), may hold values from 1 to 16, as said below
- neighbours: int32 [16384, 16], P('nodes'), may hold values from 0 to 255
- served_rows: int32 [256, 16], P('nodes'), may hold values from 0 to 1023
- label_mask: int32 [16384], P('nodes'), may hold values from 0 to 1, as said below
- targets: float32 [16384, 128], P('nodes'), may hold values from -6 to 6
- embed_weight: float32 [128, 256], P(None, 'tower'), may hold values from -0.5 to 0.5
- pre_weight: float32 [2, 528, 256], P(None, None, 'tower'), may hold values from -0.25 to 0.25
- post_weight: float32 [2, 4, 1024, 64], P(None, 'tower'), may hold values from -0.1875 to 0.1875
- mix_weight: float32 [2, 256, 256], P(None, 'tower'), may hold values from -0.375 to 0.375
- inner_weight: float32 [256, 256], P(None, 'tower'), may hold values from -0.375 to 0.375
- outer_weight: float32 [256, 128], P('tower'), may hold values from -0.375 to 0.375
- embed_moment: float32 [128, 256], P(None, 'tower'), may hold values from -0.0009765625 to 0.0009765625
- pre_moment: float32 [2, 528, 256], P(None, None, 'tower'), may hold values from -0.0009765625 to 0.0009765625
- post_moment: float32 [2, 4, 1024, 64], P(None, 'tower'), may hold values from -0.0009765625 to 0.0009765625
- mix_moment: float32 [2, 256, 256], P(None, 'tower'), may hold values from -0.0009765625 to 0.0009765625
- inner_moment: float32 [256, 256], P(None, 'tower'), may hold values from -0.0009765625 to 0.0009765625
- outer_moment: float32 [256, 128], P('tower'), may hold values from -0.0009765625 to 0.0009765625
Outputs:
- loss_value: float32 [], replicated
- embed_momentum: float32 [128, 256], P(None, 'tower')
- pre_momentum: float32 [2, 528, 256], P(None, None, 'tower')
- post_momentum: float32 [2, 4, 1024, 64], P(None, 'tower')
- mix_momentum: float32 [2, 256, 256], P(None, 'tower')
- inner_momentum: float32 [256, 256], P(None, 'tower')
- outer_momentum: float32 [256, 128], P('tower')
- embed_master: float32 [128, 256], P(None, 'tower')
- pre_master: float32 [2, 528, 256], P(None, None, 'tower')
- post_master: float32 [2, 4, 1024, 64], P(None, 'tower')
- mix_master: float32 [2, 256, 256], P(None, 'tower')
- inner_master: float32 [256, 256], P(None, 'tower')
- outer_master: float32 [256, 128], P('tower')
- embed_copy: bfloat16 [128, 256], P(None, 'tower')
- pre_copy: bfloat16 [2, 528, 256], P(None, None, 'tower')
- post_copy: bfloat16 [2, 4, 1024, 64], P(None, 'tower')
- mix_copy: bfloat16 [2, 256, 256], P(None, 'tower')
- inner_copy: bfloat16 [256, 256], P(None, 'tower')
- outer_copy: bfloat16 [256, 128], P('tower')
The draws below stay inside these ranges and needn't reach their ends.
Inputs may be any that keep to these rules, and one draw needn't show every extreme that they name: `degree`: the first node of every device has 16 valid slots. `label_mask`: the first node of every device has its label present.
All inputs are finite; a program needn't handle non-finite values.
Results may differ from the reference program's by a relative error of at most 0.01.
The reference program's roundings to bfloat16 on the way count: a program that leaves them out, or rounds other values in their place, can miss the bound.
Values may be sent and summed in bfloat16 or wider, within the bound.
No kernel may reach another device: no remote copies, remote signals or barrier semaphores. Data moves between devices by JAX's collectives and lax.ppermute only.
A program may use at most 128 MiB of HBM per device.

```python
import math
import jax
import jax.numpy as jnp
import numpy as np
from jax import lax

HIDDEN_WIDTH = 256
TOWERS = 4
TW = 64
EDGE = 16
FIN = 128
OUT = 128
K = 16
CAP = 16
LAYERS = 2
NODE_DEV = 1024
NODES = 16384
PAIRS = 256
N_NODES = 16


def draw_degree(key, part):
    ranks = jax.random.randint(key, (NODES,), 1, K // 2 + 1)
    values = K // ranks
    positions = jnp.arange(NODES, dtype=jnp.int32)
    return jnp.where(positions % NODE_DEV == 0, K, values).astype(jnp.int32)


def draw_label_mask(key, part):
    positions = jnp.arange(NODES, dtype=jnp.int32)
    device = positions // NODE_DEV
    threshold = 256 + 512 * device // max(N_NODES - 1, 1)
    draws = jax.random.randint(key, (NODES,), 0, 1024)
    present = (draws < threshold) | (positions % NODE_DEV == 0)
    return jnp.where(present, 1, 0).astype(jnp.int32)


def place_ends(array, rng, low, top_value):
    longest = array.shape.index(max(array.shape))
    spots = []
    for shift in (0, 1):
        where = [jax.random.randint(jax.random.fold_in(rng, axis), (), 0, length) for axis, length in enumerate(array.shape)]
        where[longest] = (where[longest] + shift) % array.shape[longest]
        spots.append(tuple(where))
    return array.at[spots[0]].set(low).at[spots[1]].set(top_value)


def levels(own_key, extent, split, least, top_value):
    loudness = 1.0
    for position, blocks in split:
        steps = jax.random.uniform(jax.random.fold_in(jax.random.fold_in(own_key, 6), position), (blocks,), jnp.float32, least / len(split), top_value / len(split))
        loudness = loudness * jnp.repeat(jnp.exp(steps), extent[position] // blocks).reshape((-1,) + (1,) * (len(extent) - 1 - position))
    return loudness


def cumulative_ranks(amount, slope):
    weights = [(1 << 20) // math.isqrt(rank ** slope) + 1 for rank in range(1, amount + 1)]
    scale = 1 + sum(weights) // (1 << 30)
    return np.cumsum(np.array([max(1, weight // scale) for weight in weights]))


def skewed_ids(own_key, dims, count, lean):
    table = cumulative_ranks(count, lean)
    pick = jax.random.randint(jax.random.fold_in(own_key, 1), dims, 0, int(table[count - 1]))
    grade = jnp.searchsorted(jnp.asarray(table, jnp.int32), pick, side="right")
    return jax.random.permutation(jax.random.fold_in(own_key, 2), count)[grade].astype(jnp.int32)


def scatter_about(stream_key, extent, scale, reach, split=(), kind=jnp.bfloat16):
    gain = levels(stream_key, extent, split, -0.22, 0.18) if split else 1.0
    array = jax.random.normal(stream_key, extent, jnp.float32) * scale * gain
    return jnp.minimum(jnp.maximum(array, -reach), reach).astype(kind)


def setup_inputs(seed: int = 0) -> dict:
    key_of = jax.random.split(jax.random.key(seed), 20)
    features = scatter_about(key_of[0], (NODES, FIN), 1.0, 6.0, ((0, 16),))
    edge_values = scatter_about(key_of[1], (NODES, K * EDGE), 1.0, 6.0, ((0, 16),))
    degree = draw_degree(jax.random.fold_in(key_of[19], 71), 0)
    neighbours = place_ends(jax.random.randint(key_of[3], (NODES, K), 0, N_NODES * CAP), jax.random.fold_in(key_of[3], 1), 0, (N_NODES * CAP) - 1).astype(jnp.int32)
    served_rows = place_ends(skewed_ids(key_of[4], (PAIRS, CAP), NODE_DEV, 2), jax.random.fold_in(key_of[4], 3), 0, NODE_DEV - 1).astype(jnp.int32)
    label_mask = draw_label_mask(jax.random.fold_in(key_of[19], 71), 0)
    targets = scatter_about(key_of[6], (NODES, OUT), 1.0, 6.0, ((0, 16),), jnp.float32)
    embed_weight = scatter_about(key_of[7], (FIN, HIDDEN_WIDTH), FIN ** -0.5, 0.5, ((1, 2),), jnp.float32)
    pre_weight = scatter_about(key_of[8], (LAYERS, 2 * HIDDEN_WIDTH + EDGE, HIDDEN_WIDTH), (2 * HIDDEN_WIDTH + EDGE) ** -0.5, 0.25, ((2, 2),), jnp.float32)
    post_weight = scatter_about(key_of[9], (LAYERS, TOWERS, HIDDEN_WIDTH + 12 * TW, TW), (HIDDEN_WIDTH + 12 * TW) ** -0.5, 0.1875, ((1, 2),), jnp.float32)
    mix_weight = scatter_about(key_of[10], (LAYERS, HIDDEN_WIDTH, HIDDEN_WIDTH), HIDDEN_WIDTH ** -0.5, 0.375, ((1, 2),), jnp.float32)
    inner_weight = scatter_about(key_of[11], (HIDDEN_WIDTH, HIDDEN_WIDTH), HIDDEN_WIDTH ** -0.5, 0.375, ((1, 2),), jnp.float32)
    outer_weight = scatter_about(key_of[12], (HIDDEN_WIDTH, OUT), HIDDEN_WIDTH ** -0.5, 0.375, ((0, 2),), jnp.float32)
    embed_moment = scatter_about(key_of[13], (FIN, HIDDEN_WIDTH), (3.0 / (OUT * (NODE_DEV * N_NODES) ** 0.5)), 0.0009765625, ((1, 2),), jnp.float32)
    pre_moment = scatter_about(key_of[14], (LAYERS, 2 * HIDDEN_WIDTH + EDGE, HIDDEN_WIDTH), (3.0 / (OUT * (NODE_DEV * N_NODES) ** 0.5)), 0.0009765625, ((2, 2),), jnp.float32)
    post_moment = scatter_about(key_of[15], (LAYERS, TOWERS, HIDDEN_WIDTH + 12 * TW, TW), (3.0 / (OUT * (NODE_DEV * N_NODES) ** 0.5)), 0.0009765625, ((1, 2),), jnp.float32)
    mix_moment = scatter_about(key_of[16], (LAYERS, HIDDEN_WIDTH, HIDDEN_WIDTH), (3.0 / (OUT * (NODE_DEV * N_NODES) ** 0.5)), 0.0009765625, ((1, 2),), jnp.float32)
    inner_moment = scatter_about(key_of[17], (HIDDEN_WIDTH, HIDDEN_WIDTH), (3.0 / (OUT * (NODE_DEV * N_NODES) ** 0.5)), 0.0009765625, ((1, 2),), jnp.float32)
    outer_moment = scatter_about(key_of[18], (HIDDEN_WIDTH, OUT), (3.0 / (OUT * (NODE_DEV * N_NODES) ** 0.5)), 0.0009765625, ((0, 2),), jnp.float32)
    return {"features": features, "edge_values": edge_values, "degree": degree, "neighbours": neighbours, "served_rows": served_rows, "label_mask": label_mask, "targets": targets, "embed_weight": embed_weight, "pre_weight": pre_weight, "post_weight": post_weight, "mix_weight": mix_weight, "inner_weight": inner_weight, "outer_weight": outer_weight, "embed_moment": embed_moment, "pre_moment": pre_moment, "post_moment": post_moment, "mix_moment": mix_moment, "inner_moment": inner_moment, "outer_moment": outer_moment}


MATMUL_ACCURACY = lax.Precision.HIGHEST
DEGREE_SCALE = 1.5
NEWTON_A = 3.4445
NEWTON_B = -4.775
NEWTON_C = 2.0315
LEARN_RATE = 0.3
MOMENT_DECAY = 0.5
NORM_FLOOR = 1e-07

@jax.custom_vjp
def low(v):
    return lax.optimization_barrier(v.astype(jnp.bfloat16)).astype(jnp.float32)

@jax.custom_vjp
def low_back(v):
    return v

def low_keep(v):
    return (low(v), None)

def low_pass(kept, grad):
    return (grad,)

def back_keep(v):
    return (v, None)

def back_low(kept, grad):
    return (low(grad),)
low.defvjp(low_keep, low_pass)
low_back.defvjp(back_keep, back_low)

def product(a, b):
    return jnp.dot(a, b, precision=MATMUL_ACCURACY)

def aggregate(m, degree, width):
    slot_count = m.shape[1]
    slot_ids = jnp.arange(slot_count, dtype=jnp.int32)
    valid = (slot_ids[None, :] < degree[:, None])[:, :, None]
    valid_slot = valid.astype(m.dtype)
    degree_float = degree.astype(m.dtype)[:, None]
    average = lax.optimization_barrier(jnp.sum(m * valid_slot, axis=1)) / degree_float
    variance = lax.optimization_barrier(jnp.sum(valid_slot * (m - average[:, None, :]) ** 2, axis=1)) / degree_float
    spread = jnp.sqrt(variance + 1.0)
    largest = lax.optimization_barrier(jnp.max(jnp.where(valid, m, -jnp.inf), axis=1))
    smallest = lax.optimization_barrier(jnp.min(jnp.where(valid, m, jnp.inf), axis=1))
    log_degree = jnp.log(degree_float + 1.0)
    node_count = m.shape[0]
    towers_here = m.shape[2] // width
    statistics = jnp.stack([average, smallest, largest, spread], axis=1).reshape(node_count, 4, towers_here, width)
    scaled = jnp.stack([statistics, statistics * (log_degree / DEGREE_SCALE)[:, :, None, None], statistics * (DEGREE_SCALE / log_degree)[:, :, None, None]], axis=1)
    return scaled.transpose(0, 3, 1, 2, 4).reshape(node_count, towers_here, 12 * width)

def forward(params, features, edge_values, degree, source_node, label_mask, targets):
    embed, pre, post, mix, inner, outer = params
    h = low_back(product(features, low(embed)))
    node_count = h.shape[0]
    edge_slots = edge_values.reshape(node_count, K, EDGE)
    for l in range(LAYERS):
        h_narrow = low(h)
        weights = low(pre[l])
        target_part = low_back(product(h_narrow, weights[:HIDDEN_WIDTH]))
        source_part = low(low_back(product(h_narrow, weights[HIDDEN_WIDTH:2 * HIDDEN_WIDTH])))
        edge_part = low_back(jnp.einsum('nke,ec->nkc', edge_slots, weights[2 * HIDDEN_WIDTH:], precision=MATMUL_ACCURACY))
        m = target_part[:, None, :] + source_part[source_node] + edge_part
        pooled_nodes = low(aggregate(m, degree, TW))
        post_reduced = low(post[l])
        layer_output = jnp.einsum('nh,thc->ntc', h_narrow, post_reduced[:, :HIDDEN_WIDTH], precision=MATMUL_ACCURACY)
        layer_output = layer_output + jnp.einsum('rei,eis->res', pooled_nodes, post_reduced[:, HIDDEN_WIDTH:], precision=MATMUL_ACCURACY)
        layer_output = low(low_back(layer_output.reshape(node_count, HIDDEN_WIDTH)))
        z = low_back(product(layer_output, low(mix[l])))
        h = h + jax.nn.silu(z)
    h_narrow = low(h)
    hidden = low(jax.nn.silu(low_back(product(h_narrow, low(inner)))))
    prediction = low_back(product(hidden, low(outer)))
    error_rows = prediction - targets
    label_float = label_mask.astype(prediction.dtype)
    present = jnp.sum(label_float)
    return jnp.sum(label_float * lax.optimization_barrier(jnp.mean(error_rows * error_rows, axis=1))) / present

def orthogonal(M, on_left):
    X = M / (jnp.sqrt(jnp.sum(M * M)) + NORM_FLOOR)
    for _ in range(5):
        if on_left:
            A = product(X, X.T)
            X = NEWTON_A * X + product(NEWTON_B * A + NEWTON_C * product(A, A), X)
        else:
            A = product(X.T, X)
            X = NEWTON_A * X + product(X, NEWTON_B * A + NEWTON_C * product(A, A))
    return X

def reference(features, edge_values, degree, neighbours, served_rows, label_mask, targets, embed_weight, pre_weight, post_weight, mix_weight, inner_weight, outer_weight, embed_moment, pre_moment, post_moment, mix_moment, inner_moment, outer_moment):
    served = served_rows.reshape(N_NODES, N_NODES, CAP)
    owners = jnp.arange(N_NODES, dtype=jnp.int32)[:, None, None] * NODE_DEV + served
    by_requester = owners.transpose(1, 0, 2).reshape(N_NODES, N_NODES * CAP)
    device_of = jnp.arange(N_NODES * NODE_DEV, dtype=jnp.int32) // NODE_DEV
    source_node = by_requester[device_of[:, None], neighbours]
    feats = features.astype(jnp.float32)
    edges = edge_values.astype(jnp.float32)
    params = (embed_weight, pre_weight, post_weight, mix_weight, inner_weight, outer_weight)

    def objective(*weights):
        return forward(weights, feats, edges, degree, source_node, label_mask, targets)
    loss_value, pullback = jax.vjp(objective, *params)
    gradients = pullback(jnp.ones_like(loss_value))
    previous = (embed_moment, pre_moment, post_moment, mix_moment, inner_moment, outer_moment)
    moments = tuple((MOMENT_DECAY * p + g for p, g in zip(previous, gradients)))
    left_flags = (True, True, False, False, True, False)
    directions = []
    for moment, on_left in zip(moments, left_flags):
        flat = moment.reshape((-1,) + moment.shape[-2:])
        result = jax.vmap(lambda q: orthogonal(q, on_left))(flat)
        directions.append(result.reshape(moment.shape))
    masters = []
    for weight, direction in zip(params, directions):
        factor = math.sqrt(max(1.0, weight.shape[-2] / weight.shape[-1]))
        masters.append(weight - LEARN_RATE * factor * direction)
    copies = [w.astype(jnp.bfloat16) for w in masters]
    return (loss_value, moments[0], moments[1], moments[2], moments[3], moments[4], moments[5], masters[0], masters[1], masters[2], masters[3], masters[4], masters[5], copies[0], copies[1], copies[2], copies[3], copies[4], copies[5])
```

```python
import math

import jax
import jax.numpy as jnp
from jax import lax
from jax.sharding import PartitionSpec as P

HIDDEN_WIDTH = 256
TW = 64
EDGE = 16
FIN = 128
OUT = 128
K = 16
CAP = 16
LAYERS = 2


MATMUL_ACCURACY = lax.Precision.HIGH
DEGREE_SCALE = 1.5
NEWTON_A = 3.4445
NEWTON_B = -4.775
NEWTON_C = 2.0315
LEARN_RATE = 0.3
MOMENT_DECAY = 0.5
NORM_FLOOR = 1e-07
SLOT_BLOCK = 8192


def for_sending(x):
    return jax.tree.map(lambda a: a.astype(jnp.bfloat16) if a.dtype == jnp.float32 else a, x)


def product(a, b):
    return jnp.dot(a, b, preferred_element_type=jnp.float32)


def contract_inner(form, a, b):
    return jnp.einsum(form, a, b, preferred_element_type=jnp.float32)


def swap(x):
    return lax.ppermute(x, "tower", [(0, 1), (1, 0)])


COLOURS = 3


def node_total(x):
    n = lax.axis_size("nodes")
    bits = n.bit_length() - 1
    place = lax.axis_index("nodes")
    size = x.shape[0]
    unit = COLOURS * n * 1024
    rows = -(-size // unit) * unit // 128
    padded = jnp.pad(x, (0, rows * 128 - size)).reshape(COLOURS, rows // COLOURS, 128)
    orders = [[(c + k) % bits for k in range(bits)] for c in range(COLOURS)]
    pieces = [padded[c] for c in range(COLOURS)]

    def partner(b):
        return [(i, i ^ (1 << b)) for i in range(n)]

    for k in range(bits):
        sent, kept = ([], [])
        for c in range(COLOURS):
            mine = (place >> orders[c][k]) & 1
            half = pieces[c].shape[0] // 2
            sent.append(lax.dynamic_slice_in_dim(pieces[c], (1 - mine) * half, half, 0))
            kept.append(lax.dynamic_slice_in_dim(pieces[c], mine * half, half, 0))
        got = [lax.ppermute(v, "nodes", partner(orders[c][k])) for c, v in enumerate(sent)]
        pieces = [u + v for u, v in zip(kept, got)]
    for k in reversed(range(bits)):
        got = [lax.ppermute(v, "nodes", partner(orders[c][k])) for c, v in enumerate(pieces)]
        joined = []
        for c in range(COLOURS):
            mine = (place >> orders[c][k]) & 1
            first = jnp.where(mine == 0, pieces[c], got[c])
            second = jnp.where(mine == 0, got[c], pieces[c])
            joined.append(jnp.concatenate([first, second], axis=0))
        pieces = joined
    return jnp.concatenate(pieces, axis=0).reshape(-1)[:size]


def silu_slope(z):
    sigma = jax.nn.sigmoid(z)
    return sigma * (1.0 + z * (1.0 - sigma))


def pick_rows(index, table):
    count = index.shape[0]
    block = min(count, SLOT_BLOCK)
    blocks = index.reshape(count // block, block)
    row_ids = jnp.arange(table.shape[0], dtype=jnp.int32)

    def select(part):
        chooser = (part[:, None] == row_ids[None, :]).astype(jnp.bfloat16)
        return product(chooser, table).astype(jnp.bfloat16)

    return lax.map(select, blocks).reshape(count, table.shape[1])


def add_rows(index, values, rows):
    count = index.shape[0]
    block = min(count, SLOT_BLOCK)
    upper = values.astype(jnp.bfloat16)
    lower = (values - upper.astype(jnp.float32)).astype(jnp.bfloat16)
    blocks = (
        index.reshape(count // block, block),
        upper.reshape(count // block, block, -1),
        lower.reshape(count // block, block, -1),
    )
    row_ids = jnp.arange(rows, dtype=jnp.int32)

    def accumulate(total, piece):
        part, high_part, low_part = piece
        chooser = (part[:, None] == row_ids[None, :]).astype(jnp.bfloat16)
        total = total + contract_inner("nr,nc->rc", chooser, high_part)
        return (total + contract_inner("nr,nc->rc", chooser, low_part), None)

    total, _ = lax.scan(accumulate, jnp.zeros((rows, values.shape[1]), jnp.float32), blocks)
    return total


def aggregate(m, degree, width):
    slot_count = m.shape[1]
    slot_ids = jnp.arange(slot_count, dtype=jnp.int32)
    valid = (slot_ids[None, :] < degree[:, None])[:, :, None]
    valid_slot = valid.astype(jnp.float32)
    degree_float = degree.astype(jnp.float32)[:, None]
    average = jnp.sum(m * valid_slot, axis=1) / degree_float
    variance = jnp.sum(valid_slot * (m - average[:, None, :]) ** 2, axis=1) / degree_float
    spread = jnp.sqrt(variance + 1.0)
    largest = jnp.max(jnp.where(valid, m, -jnp.inf), axis=1)
    smallest = jnp.min(jnp.where(valid, m, jnp.inf), axis=1)
    log_degree = jnp.log(degree_float + 1.0)
    node_count = m.shape[0]
    towers_here = m.shape[2] // width
    statistics = jnp.stack([average, smallest, largest, spread], axis=1).reshape(
        node_count, 4, towers_here, width
    )
    scaled = jnp.stack(
        [
            statistics,
            statistics * (log_degree / DEGREE_SCALE)[:, :, None, None],
            statistics * (DEGREE_SCALE / log_degree)[:, :, None, None],
        ],
        axis=1,
    )
    return scaled.transpose(0, 3, 1, 2, 4).reshape(node_count, towers_here, 12 * width)


def messages(h_narrow, weights, edge_slots, incoming, neighbours):
    node_count = h_narrow.shape[0]
    target_part = product(h_narrow, weights[:HIDDEN_WIDTH])
    edge_part = contract_inner("nke,ec->nkc", edge_slots, weights[2 * HIDDEN_WIDTH :])
    fetched = pick_rows(neighbours.reshape(-1), incoming).reshape(
        node_count, neighbours.shape[1], -1
    )
    return target_part[:, None, :] + fetched.astype(jnp.float32) + edge_part


def tower_outputs(h_narrow, pooled_reduced, post_reduced):
    layer_output = contract_inner("nh,thc->ntc", h_narrow, post_reduced[:, :HIDDEN_WIDTH])
    layer_output = layer_output + contract_inner(
        "rei,eis->res", pooled_reduced, post_reduced[:, HIDDEN_WIDTH:]
    )
    return layer_output.reshape(h_narrow.shape[0], -1).astype(jnp.bfloat16)


def layer_forward(
    h, weights, post_reduced, mix_narrow, edge_slots, degree, neighbours, served_rows
):
    h_narrow = h.astype(jnp.bfloat16)
    source_part = product(h_narrow, weights[HIDDEN_WIDTH : 2 * HIDDEN_WIDTH]).astype(jnp.bfloat16)
    outgoing = pick_rows(served_rows.reshape(-1), source_part).reshape(
        served_rows.shape[0], served_rows.shape[1], -1
    )
    incoming = lax.all_to_all(outgoing, "nodes", split_axis=0, concat_axis=0, tiled=True)
    incoming = incoming.reshape(-1, incoming.shape[2])
    m = messages(h_narrow, weights, edge_slots, incoming, neighbours)
    pooled_nodes = aggregate(m, degree, TW).astype(jnp.bfloat16)
    y_narrow = tower_outputs(h_narrow, pooled_nodes, post_reduced)
    part = product(y_narrow, mix_narrow)
    z = part + swap(part)
    return (h + jax.nn.silu(z), incoming, z)


def both(x):
    narrow = x.astype(jnp.bfloat16)
    return narrow.astype(jnp.float32) + swap(narrow).astype(jnp.float32)


def layer_backward(
    h_grad,
    h,
    incoming,
    z,
    weights,
    post_reduced,
    mix_narrow,
    edge_slots,
    degree,
    neighbours,
    served_rows,
):
    node_count = h.shape[0]
    h_narrow = h.astype(jnp.bfloat16)
    m = messages(h_narrow, weights, edge_slots, incoming, neighbours)
    pooled_nodes, pooled_backward = jax.vjp(lambda v: aggregate(v, degree, TW), m)
    pooled_reduced = pooled_nodes.astype(jnp.bfloat16)
    y_narrow = tower_outputs(h_narrow, pooled_reduced, post_reduced)
    z_grad = (h_grad * silu_slope(z)).astype(jnp.bfloat16)
    grad_mix = contract_inner("nr,nc->rc", y_narrow, z_grad)
    output_gradient = contract_inner("nc,rc->nr", z_grad, mix_narrow).astype(jnp.bfloat16)
    output_gradient = output_gradient.reshape(node_count, post_reduced.shape[0], TW)
    grad_post = jnp.concatenate(
        [
            contract_inner("nh,ntc->thc", h_narrow, output_gradient),
            contract_inner("uli,ulr->lir", pooled_reduced, output_gradient),
        ],
        axis=1,
    )
    back_h = contract_inner("ntc,thc->nh", output_gradient, post_reduced[:, :HIDDEN_WIDTH])
    (moment_gradient,) = pooled_backward(
        contract_inner("hpj,pkj->hpk", output_gradient, post_reduced[:, HIDDEN_WIDTH:])
    )
    target_grad = jnp.sum(moment_gradient, axis=1).astype(jnp.bfloat16)
    edge_grad = contract_inner("nke,nkc->ec", edge_slots, moment_gradient.astype(jnp.bfloat16))
    columns = moment_gradient.shape[2]
    fetched_grad = add_rows(
        neighbours.reshape(-1), moment_gradient.reshape(-1, columns), incoming.shape[0]
    )
    returned = lax.all_to_all(
        fetched_grad.reshape(-1, CAP, columns).astype(jnp.bfloat16),
        "nodes",
        split_axis=0,
        concat_axis=0,
        tiled=True,
    ).astype(jnp.float32)
    source_grad = add_rows(
        served_rows.reshape(-1), returned.reshape(-1, columns), node_count
    ).astype(jnp.bfloat16)
    grad_pre = jnp.concatenate(
        [
            contract_inner("nh,nc->hc", h_narrow, target_grad),
            contract_inner("nh,nc->hc", h_narrow, source_grad),
            edge_grad,
        ],
        axis=0,
    )
    back_h = back_h + contract_inner("nc,hc->nh", target_grad, weights[:HIDDEN_WIDTH])
    back_h = back_h + contract_inner(
        "nc,hc->nh", source_grad, weights[HIDDEN_WIDTH : 2 * HIDDEN_WIDTH]
    )
    return (
        h_grad + both(back_h),
        grad_pre,
        grad_post,
        grad_mix,
    )


def gram_local(X, on_left):
    if on_left:
        return jnp.einsum("...ij,...kj->...ik", X, X, precision=MATMUL_ACCURACY)
    return jnp.einsum("...ji,...jk->...ik", X, X, precision=MATMUL_ACCURACY)


def newton_step(X, A, on_left):
    poly = NEWTON_B * A + NEWTON_C * jnp.einsum(
        "...ij,...jk->...ik", A, A, precision=MATMUL_ACCURACY
    )
    if on_left:
        return NEWTON_A * X + jnp.einsum("...ij,...jk->...ik", poly, X, precision=MATMUL_ACCURACY)
    return NEWTON_A * X + jnp.einsum("...ij,...jk->...ik", X, poly, precision=MATMUL_ACCURACY)


def newton_local(M):
    X = M / (jnp.sqrt(jnp.sum(M * M, axis=(-2, -1))) + NORM_FLOOR)[..., None, None]
    for _ in range(5):
        X = newton_step(X, gram_local(X, False), False)
    return X


def body(
    features,
    edge_values,
    degree,
    neighbours,
    served_rows,
    label_mask,
    targets,
    embed_weight,
    pre_weight,
    post_weight,
    mix_weight,
    inner_weight,
    outer_weight,
    embed_moment,
    pre_moment,
    post_moment,
    mix_moment,
    inner_moment,
    outer_moment,
):
    node_count = features.shape[0]
    edge_slots = edge_values.reshape(node_count, K, EDGE)
    share_cols = embed_weight.shape[1]
    offset = lax.axis_index("tower") * share_cols
    h = lax.all_gather(
        product(features, embed_weight.astype(jnp.bfloat16)), "tower", axis=1, tiled=True
    )
    pre_narrow = pre_weight.astype(jnp.bfloat16)
    post_reduced = post_weight.astype(jnp.bfloat16)
    mix_narrow = mix_weight.astype(jnp.bfloat16)
    stored = []
    for l in range(LAYERS):
        h_next, incoming, z = layer_forward(
            h,
            pre_narrow[l],
            post_reduced[l],
            mix_narrow[l],
            edge_slots,
            degree,
            neighbours,
            served_rows,
        )
        stored.append((h, incoming, z))
        h = h_next
    inner_narrow = inner_weight.astype(jnp.bfloat16)
    outer_narrow = outer_weight.astype(jnp.bfloat16)
    h_narrow = h.astype(jnp.bfloat16)
    inner_pre = product(h_narrow, inner_narrow)
    hidden = jax.nn.silu(inner_pre).astype(jnp.bfloat16)
    prediction = both(product(hidden, outer_narrow))
    error_rows = prediction - targets
    label_float = label_mask.astype(jnp.float32)
    loss_sum = jnp.sum(label_float * jnp.mean(error_rows * error_rows, axis=1))
    present_here = jnp.sum(label_float)
    pred_grad = (2.0 * error_rows * label_float[:, None] / OUT).astype(jnp.bfloat16)
    grad_outer = contract_inner("nh,no->ho", hidden, pred_grad)
    inner_grad = (
        contract_inner("no,ho->nh", pred_grad, outer_narrow) * silu_slope(inner_pre)
    ).astype(jnp.bfloat16)
    grad_inner = contract_inner("nh,nc->hc", h_narrow, inner_grad)
    h_grad = both(contract_inner("nc,hc->nh", inner_grad, inner_narrow))
    pre_list = [None] * LAYERS
    post_list = [None] * LAYERS
    mix_list = [None] * LAYERS
    for l in reversed(range(LAYERS)):
        h_prev, incoming, z = stored[l]
        h_grad, pre_list[l], post_list[l], mix_list[l] = layer_backward(
            h_grad,
            h_prev,
            incoming,
            z,
            pre_narrow[l],
            post_reduced[l],
            mix_narrow[l],
            edge_slots,
            degree,
            neighbours,
            served_rows,
        )
    cols_grad = lax.dynamic_slice_in_dim(h_grad.astype(jnp.bfloat16), offset, share_cols, 1)
    grad_embed = contract_inner("nf,nc->fc", features, cols_grad)
    parts = (
        grad_embed,
        jnp.stack(pre_list),
        jnp.stack(post_list),
        jnp.stack(mix_list),
        grad_inner,
        grad_outer,
    )
    flat = node_total(jnp.concatenate([part.reshape(-1) for part in parts]))
    loss_sum, present = jnp.sum(
        lax.all_gather(jnp.stack([loss_sum, present_here]), "nodes", axis=0), axis=0
    )
    loss_value = loss_sum / present
    gradients = []
    start = 0
    for part in parts:
        stop = start + math.prod(part.shape)
        gradients.append(flat[start:stop].reshape(part.shape) / present)
        start = stop
    previous = (embed_moment, pre_moment, post_moment, mix_moment, inner_moment, outer_moment)
    moments = [MOMENT_DECAY * p + g for p, g in zip(previous, gradients)]
    split_dims = (1, 2, None, 1, 1, 0)
    directions = []
    for moment, dim in zip(moments, split_dims):
        if dim is None:
            directions.append(newton_local(moment))
            continue
        full = jnp.concatenate([moment, swap(moment)], axis=dim)
        tall = full.shape[-2] >= full.shape[-1]
        if not tall:
            full = jnp.swapaxes(full, -1, -2)
        done = newton_local(full)
        if not tall:
            done = jnp.swapaxes(done, -1, -2)
        directions.append(lax.slice_in_dim(done, 0, moment.shape[dim], axis=dim))
    whole_shapes = [
        (FIN, HIDDEN_WIDTH),
        (2 * HIDDEN_WIDTH + EDGE, HIDDEN_WIDTH),
        (HIDDEN_WIDTH + 12 * TW, TW),
        (HIDDEN_WIDTH, HIDDEN_WIDTH),
        (HIDDEN_WIDTH, HIDDEN_WIDTH),
        (HIDDEN_WIDTH, OUT),
    ]
    params = (embed_weight, pre_weight, post_weight, mix_weight, inner_weight, outer_weight)
    masters = []
    for weight, direction, dims in zip(params, directions, whole_shapes):
        factor = math.sqrt(max(1.0, dims[0] / dims[1]))
        masters.append(weight - LEARN_RATE * factor * direction)
    copies = [w.astype(jnp.bfloat16) for w in masters]
    return (
        loss_value,
        moments[0],
        moments[1],
        moments[2],
        moments[3],
        moments[4],
        moments[5],
        masters[0],
        masters[1],
        masters[2],
        masters[3],
        masters[4],
        masters[5],
        copies[0],
        copies[1],
        copies[2],
        copies[3],
        copies[4],
        copies[5],
    )


def solution(mesh):
    return jax.shard_map(
        body,
        mesh=mesh,
        in_specs=(
            P("nodes", None),
            P("nodes", None),
            P("nodes"),
            P("nodes", None),
            P("nodes", None),
            P("nodes"),
            P("nodes", None),
            P(None, "tower"),
            P(None, None, "tower"),
            P(None, "tower", None, None),
            P(None, "tower", None),
            P(None, "tower"),
            P("tower", None),
            P(None, "tower"),
            P(None, None, "tower"),
            P(None, "tower", None, None),
            P(None, "tower", None),
            P(None, "tower"),
            P("tower", None),
        ),
        out_specs=(
            P(),
            P(None, "tower"),
            P(None, None, "tower"),
            P(None, "tower", None, None),
            P(None, "tower", None),
            P(None, "tower"),
            P("tower", None),
            P(None, "tower"),
            P(None, None, "tower"),
            P(None, "tower", None, None),
            P(None, "tower", None),
            P(None, "tower"),
            P("tower", None),
            P(None, "tower"),
            P(None, None, "tower"),
            P(None, "tower", None, None),
            P(None, "tower", None),
            P(None, "tower"),
            P("tower", None),
        ),
        check_vma=False,
    )
```
